32 devices in a mesh: group: 2 (over y), src: 4 (over z), rcv: 4 (over x, core).
Axes of the slice: x: 2, y: 2, z: 4, core: 2. Of those that a mesh axis runs over, the one named last changes fastest.
Arguments:
- traces: bfloat16 [128, 36864], P(('group', 'src', 'rcv')), parts along dimension 0, may hold values from -6 to 6
- offsets: int32 [16], P('group'), parts along dimension 0, may hold values from 0 to 32768
- receiver_slots: int32 [8, 16], P(('group', 'rcv')), parts along dimension 0, may hold values from 0 to 15, each once within a row
Outputs:
- correlations: bfloat16 [128, 64, 128], P(('group', 'src'), 'rcv'), parts along dimension 0
The draws below stay inside these ranges and needn't reach their ends.
There are 2 independent parts, one for each index of `group`. The reference program is written for one: setup_inputs(seed, part) draws one part's arguments, and reference() takes and returns one part's arrays. A program takes and returns all parts, laid end to end along the dimension named above; each array names one. Nothing has to cross between parts.
All inputs are finite; a program needn't handle non-finite values.
Results may differ from the reference program's by a relative error of at most 0.0065.
Values may be sent and summed in bfloat16 or wider, within the bound.
No kernel may reach another device: no remote copies, remote signals or barrier semaphores. Data moves between devices by JAX's collectives and lax.ppermute only.
A program may use at most 64 MiB of HBM per device.

```python
import math
import jax
import jax.numpy as jnp
from jax import lax

SEG_LEN = 4096
NB = 512
LAGS = 128
LAG_STEP = 4
SEGS = 8
CH_DEV = 4
WIN = 36864
SB = 16
RB = 16
CHANNELS = 64
N_RCV = 4


def place_ends(drawn, stream_key, smallest, high):
    spot = [jax.random.randint(jax.random.fold_in(stream_key, axis), (), 0, length) for axis, length in enumerate(drawn.shape)]
    longest = drawn.shape.index(max(drawn.shape))
    neighbour = spot[:longest] + [(spot[longest] + 1) % drawn.shape[longest]] + spot[longest + 1:]
    return drawn.at[tuple(spot)].set(smallest).at[tuple(neighbour)].set(high)


def shard_levels(key, shape, shards, low, top_value):
    def one(dim, shards_of):
        heights = jax.random.uniform(jax.random.fold_in(jax.random.fold_in(key, 6), dim), (shards_of,), jnp.float32, low / len(shards), top_value / len(shards))
        return jnp.repeat(jnp.exp(heights), shape[dim] // shards_of).reshape((-1,) + (1,) * (len(shape) - dim - 1))

    loudness = one(*shards[0])
    for cut in shards[1:]:
        loudness = loudness * one(*cut)
    return loudness


def centred(key, shape, spread, most, split=(), held_as=jnp.bfloat16):
    array = jax.random.normal(key, shape, jnp.float32) * spread
    if len(split) > 0:
        array = shard_levels(key, shape, split, -0.22, 0.18) * array
    return jnp.clip(array, min=-most, max=most).astype(held_as)


def setup_inputs(seed: int = 0, part: int = 0) -> dict:
    key_of = jax.random.split(jax.random.key(seed), 4)
    own_keys = jax.random.split(jax.random.fold_in(key_of[3], part), 4)
    traces = centred(own_keys[0], (CHANNELS, WIN), 1.0, 6.0, ((0, 16),))
    offsets = place_ends(jax.random.randint(own_keys[1], (SEGS,), 0, SEG_LEN * SEGS + 1), jax.random.fold_in(own_keys[1], 1), 0, SEG_LEN * SEGS).astype(jnp.int32)
    receiver_slots = jax.vmap(lambda own: jax.random.permutation(own, RB))(jax.random.split(own_keys[2], N_RCV)).reshape((N_RCV, RB)).astype(jnp.int32)
    return {"traces": traces, "offsets": offsets, "receiver_slots": receiver_slots}


def dft_table():
    t_index = jnp.arange(SEG_LEN, dtype=jnp.int32)[:, None]
    k_index = jnp.arange(NB, dtype=jnp.int32)[None, :]
    phase = jnp.mod(t_index * k_index, SEG_LEN).astype(jnp.float32) * (2.0 * math.pi / SEG_LEN)
    return jnp.concatenate([jnp.cos(phase), -jnp.sin(phase)], axis=1).astype(jnp.bfloat16)

def lag_table():
    k_index = jnp.arange(NB, dtype=jnp.int32)[:, None]
    lag_shift = LAG_STEP * (jnp.arange(LAGS, dtype=jnp.int32)[None, :] - LAGS // 2)
    phase = jnp.mod(k_index * lag_shift, SEG_LEN).astype(jnp.float32) * (2.0 * math.pi / SEG_LEN)
    return jnp.concatenate([jnp.cos(phase), -jnp.sin(phase)], axis=0).astype(jnp.bfloat16)

def whiten(traces, offsets):
    table = dft_table().astype(jnp.float32)
    pieces = jax.vmap(lambda start: lax.dynamic_slice_in_dim(traces, start, SEG_LEN, 1))(offsets)
    pieces = jnp.transpose(pieces, (1, 0, 2)).reshape(-1, SEG_LEN).astype(jnp.float32)
    spectra = jnp.dot(pieces, table, precision=lax.Precision.HIGHEST, preferred_element_type=jnp.float32)
    energy = lax.optimization_barrier(jnp.mean(spectra * spectra, axis=-1, keepdims=True))
    white = (spectra / jnp.sqrt(energy + 1e-06)).astype(jnp.bfloat16)
    return white.reshape(traces.shape[0], SEGS, 2 * NB)

def block_corr(sources, receivers, lags):
    high = lax.Precision.HIGHEST
    src_re = sources[..., :NB].astype(jnp.float32)
    src_im = sources[..., NB:].astype(jnp.float32)
    rec_re = receivers[..., :NB].astype(jnp.float32)
    rec_im = receivers[..., NB:].astype(jnp.float32)

    def pair(left, right):
        return jnp.einsum('sgk,rgk->srk', left, right, precision=high)
    real_part = pair(src_re, rec_re) + pair(src_im, rec_im)
    imag_part = pair(src_re, rec_im) - pair(src_im, rec_re)
    cross = jnp.concatenate([real_part, imag_part], axis=-1).astype(jnp.bfloat16)
    out = jnp.einsum('srk,kl->srl', cross.astype(jnp.float32), lags.astype(jnp.float32), precision=high)
    return (out * (1.0 / math.sqrt(SEGS * NB))).astype(jnp.bfloat16)

def reference(traces, offsets, receiver_slots):
    white = whiten(traces, offsets)
    column = jnp.arange(CHANNELS, dtype=jnp.int32)
    block_j = column // RB
    place = receiver_slots[block_j, column % RB]
    owner_i = place // CH_DEV
    within = place % CH_DEV
    channel = (owner_i * N_RCV + block_j) * CH_DEV + within
    receivers = white[channel]
    lags = lag_table()
    grouped = white.reshape(CHANNELS // SB, SB, SEGS, 2 * NB)
    out = lax.map(lambda blk: block_corr(blk, receivers, lags), grouped)
    return out.reshape(CHANNELS, CHANNELS, LAGS)
```

```python
import functools
import math

import jax
import jax.numpy as jnp
import numpy as np
from jax import lax
from jax.experimental import pallas as pl
from jax.experimental.pallas import tpu as pltpu
from jax.sharding import PartitionSpec as P

SEG_LEN = 4096
NB = 512
LAGS = 128
LAG_STEP = 4
SEGS = 8
RADIX = 8
SUB = SEG_LEN // RADIX
QS = NB // RADIX
LANES = 128
COLS = 16


def bin_order():
    pos = np.arange(NB)
    pair, lane = pos // LANES, pos % LANES
    return RADIX * (lane % QS) + pair * (LANES // QS) + lane // QS


def sub_table():
    a = np.arange(SUB)[:, None]
    q = np.arange(QS)[None, :]
    phase = 2.0 * np.pi * ((a * q) % SUB) / SUB
    re, im = np.cos(phase), -np.sin(phase)
    top = np.concatenate([re, im], axis=1)
    low = np.concatenate([-im, re], axis=1)
    return np.concatenate([top, low], axis=0).astype(jnp.bfloat16)


def twiddles():
    r = np.arange(RADIX)[:, None]
    a = np.arange(SUB)[None, :]
    phase = 2.0 * np.pi * (r * a) / SEG_LEN
    return np.concatenate([np.cos(phase), -np.sin(phase)], axis=0).astype(np.float32)


def lag_table():
    k = bin_order()[:, None]
    tau = LAG_STEP * (np.arange(LAGS)[None, :] - LAGS // 2)
    phase = 2.0 * np.pi * ((k * tau) % SEG_LEN) / SEG_LEN
    return np.concatenate([np.cos(phase), -np.sin(phase)], axis=0).astype(jnp.bfloat16)


def real_dft8(x):
    s04, d04 = x[0] + x[4], x[0] - x[4]
    s26, d26 = x[2] + x[6], x[2] - x[6]
    s15, d15 = x[1] + x[5], x[1] - x[5]
    s37, d37 = x[3] + x[7], x[3] - x[7]
    even, odd = s04 + s26, s15 + s37
    h = math.sqrt(0.5)
    dif, tot = (d15 - d37) * h, (d15 + d37) * h
    u0, u4 = even + odd, even - odd
    u2 = (s04 - s26, s37 - s15)
    u1 = (d04 + dif, -d26 - tot)
    u3 = (d04 - dif, d26 - tot)
    conj = lambda u: (u[0], -u[1])
    return [(u0, None), u1, u2, u3, (u4, None), conj(u3), conj(u2), conj(u1)]


def spectra_kernel(off_ref, tr_hbm, table_hbm, tw_hbm, out_ref, tr, table, tw, xs, v, sems):
    chans, win = tr_hbm.shape
    rows = chans * SEGS
    copies = [
        pltpu.make_async_copy(tr_hbm, tr.at[:, pl.ds(0, win)], sems.at[0]),
        pltpu.make_async_copy(tw_hbm, tw, sems.at[1]),
        pltpu.make_async_copy(table_hbm, table, sems.at[2]),
    ]
    for c in copies:
        c.start()
    copies[0].wait()
    lane = lax.broadcasted_iota(jnp.int32, (chans, LANES), 1)
    chunks = SEG_LEN // LANES
    for g in range(SEGS):
        start = off_ref[g]
        shift = lax.rem(start, LANES)
        base = pl.multiple_of(start - shift, LANES)
        back = lax.rem(LANES - shift, LANES)
        keep = lane < LANES - shift
        prev = None
        for i in range(chunks + 1):
            piece = tr[:, pl.ds(pl.multiple_of(base + i * LANES, LANES), LANES)].astype(jnp.float32)
            now = pltpu.roll(piece, back, 1)
            if prev is not None:
                xs[pl.ds((i - 1) * rows + g, chans, stride=SEGS), :] = jnp.where(keep, prev, now)
            prev = now
    copies[1].wait()
    for h in range(rows // 16):
        for i in range(SUB // LANES):
            x = [xs[pl.ds((b * (SUB // LANES) + i) * rows + h * 16, 16), :] for b in range(RADIX)]
            for r, (re, im) in enumerate(real_dft8(x)):
                if r == 0:
                    out_re, out_im = re, jnp.zeros_like(re)
                else:
                    c = tw[pl.ds(r, 1), pl.ds(i * LANES, LANES)]
                    s = tw[pl.ds(RADIX + r, 1), pl.ds(i * LANES, LANES)]
                    if im is None:
                        out_re, out_im = re * c, re * s
                    else:
                        out_re, out_im = re * c - im * s, re * s + im * c
                v[pl.ds(r * rows + h * 16, 16), pl.ds(i * LANES, LANES)] = out_re.astype(jnp.bfloat16)
                v[pl.ds(r * rows + h * 16, 16), pl.ds(SUB + i * LANES, LANES)] = out_im.astype(jnp.bfloat16)
    copies[2].wait()
    spec = jnp.dot(v[...], table[...], preferred_element_type=jnp.float32)
    parts = [spec[r * rows : (r + 1) * rows] for r in range(RADIX)]
    total = parts[0] * parts[0]
    for part in parts[1:]:
        total = total + part * part
    energy = jnp.sum(total, axis=1, keepdims=True) * (1.0 / (2 * NB))
    scale = 1.0 / jnp.sqrt(energy + 1e-06)
    low = lax.broadcasted_iota(jnp.int32, (rows, LANES), 1) < QS
    for p in range(RADIX // 2):
        a, b = parts[2 * p] * scale, parts[2 * p + 1] * scale
        re = jnp.where(low, a, pltpu.roll(b, QS, 1))
        im = jnp.where(low, pltpu.roll(a, QS, 1), b)
        out_ref[:, pl.ds(p * LANES, LANES)] = re.astype(jnp.bfloat16)
        out_ref[:, pl.ds(NB + p * LANES, LANES)] = im.astype(jnp.bfloat16)


def spectra(traces, offsets):
    chans, win = traces.shape
    rows = chans * SEGS
    table, tw = sub_table(), twiddles()
    vmem = pl.BlockSpec(memory_space=pltpu.VMEM)
    anywhere = pl.BlockSpec(memory_space=pl.ANY)
    return pl.pallas_call(
        spectra_kernel,
        out_shape=jax.ShapeDtypeStruct((rows, 2 * NB), jnp.bfloat16),
        in_specs=[pl.BlockSpec(memory_space=pltpu.SMEM), anywhere, anywhere, anywhere],
        out_specs=vmem,
        scratch_shapes=[
            pltpu.VMEM((chans, win + LANES), jnp.bfloat16),
            pltpu.VMEM(table.shape, jnp.bfloat16),
            pltpu.VMEM(tw.shape, jnp.float32),
            pltpu.VMEM((rows * SEG_LEN // LANES, LANES), jnp.float32),
            pltpu.VMEM((RADIX * rows, 2 * SUB), jnp.bfloat16),
            pltpu.SemaphoreType.DMA((3,)),
        ],
        name="spectra",
    )(offsets, traces, jnp.asarray(table), jnp.asarray(tw))


def correlate_kernel(n_src, n_rcv, pos_ref, lags_hbm, *refs):
    sources, receivers = refs[:n_src], refs[n_src : n_src + n_rcv]
    out_ref, s_re, s_sum, s_dif, r_all, r_re, r_im, r_sum, cross, lags, sem = refs[n_src + n_rcv :]
    copy = pltpu.make_async_copy(lags_hbm, lags, sem)
    copy.start()
    first = pl.program_id(0) == 0
    s_rows = s_re.shape[0] // (NB // LANES)

    @pl.when(first)
    def _():
        for m, ref in enumerate(sources):
            rows = ref.shape[0]
            for p in range(NB // LANES):
                at = pl.ds(pl.multiple_of(p * s_rows + pos_ref[m] * rows, 16), rows)
                re = ref[:, pl.ds(p * LANES, LANES)].astype(jnp.float32)
                im = ref[:, pl.ds(NB + p * LANES, LANES)].astype(jnp.float32)
                s_re[at, :] = re
                s_sum[at, :] = re + im
                s_dif[at, :] = re - im
        for m, ref in enumerate(receivers):
            rows = ref.shape[0]
            r_all[pl.ds(m * rows, rows), :] = ref[...]

    col0 = pl.program_id(0) * COLS
    places = r_all.shape[0]
    k = lax.broadcasted_iota(jnp.int32, (COLS, places), 0)
    lane = lax.broadcasted_iota(jnp.int32, (COLS, places), 1)
    wanted = jnp.zeros((COLS, places), jnp.int32)
    for c in range(COLS):
        wanted = jnp.where(k == c, pos_ref[n_src + col0 + c] * SEGS, wanted)
    pick = jnp.concatenate(
        [jnp.where(lane == wanted + g, 1.0, 0.0).astype(jnp.bfloat16) for g in range(SEGS)], axis=0
    )
    r_re[...] = jnp.dot(pick, r_all[:, pl.ds(0, NB)], preferred_element_type=jnp.float32)
    r_im[...] = jnp.dot(pick, r_all[:, pl.ds(NB, NB)], preferred_element_type=jnp.float32)
    r_sum[...] = r_re[...] + r_im[...]

    group = 4
    groups = s_rows // SEGS // group

    def step(it, carry):
        lanes = pl.ds(pl.multiple_of(lax.div(it, groups) * LANES, LANES), LANES)
        s0 = lax.rem(it, groups) * group
        half = COLS // 2
        acc = [[[None] * 3 for _ in range(2)] for _ in range(group)]
        for g in range(SEGS):
            rec = [
                (
                    r_sum[pl.ds(g * COLS + e * half, half), lanes],
                    r_im[pl.ds(g * COLS + e * half, half), lanes],
                    r_re[pl.ds(g * COLS + e * half, half), lanes],
                )
                for e in range(2)
            ]
            for j in range(group):
                row = pl.ds(lax.div(it, groups) * s_rows + (s0 + j) * SEGS + g, half, stride=0)
                src = (s_re[row, :], s_dif[row, :], s_sum[row, :])
                for e in range(2):
                    for m in range(3):
                        term = src[m] * rec[e][m]
                        acc[j][e][m] = term if g == 0 else acc[j][e][m] + term
        for j in range(group):
            at = pl.ds(pl.multiple_of((s0 + j) * COLS, COLS), COLS)
            re = jnp.concatenate([acc[j][e][0] - acc[j][e][1] for e in range(2)], axis=0)
            im = jnp.concatenate([acc[j][e][0] - acc[j][e][2] for e in range(2)], axis=0)
            cross[at, lanes] = re.astype(jnp.bfloat16)
            lane_im = pl.ds(pl.multiple_of(NB + lax.div(it, groups) * LANES, LANES), LANES)
            cross[at, lane_im] = im.astype(jnp.bfloat16)
        return carry

    lax.fori_loop(0, groups * (NB // LANES), step, 0)
    copy.wait()
    out = jnp.dot(cross[...], lags[...], preferred_element_type=jnp.float32)
    out = (out * (1.0 / math.sqrt(SEGS * NB))).astype(jnp.bfloat16)
    out_ref[...] = out.reshape(out_ref.shape)


def correlate(sources, receivers, positions, cols):
    s_rows = sum(s.shape[0] for s in sources)
    r_rows = sum(r.shape[0] for r in receivers)
    n_out = s_rows // SEGS
    vmem = pl.BlockSpec(memory_space=pltpu.VMEM)
    f32 = jnp.float32
    return pl.pallas_call(
        functools.partial(correlate_kernel, len(sources), len(receivers)),
        out_shape=jax.ShapeDtypeStruct((n_out, cols, LAGS), jnp.bfloat16),
        grid=(cols // COLS,),
        in_specs=[pl.BlockSpec(memory_space=pltpu.SMEM), pl.BlockSpec(memory_space=pl.ANY)]
        + [vmem] * (len(sources) + len(receivers)),
        out_specs=pl.BlockSpec((n_out, COLS, LAGS), lambda t: (0, t, 0)),
        scratch_shapes=[
            pltpu.VMEM((s_rows * (NB // LANES), LANES), f32),
            pltpu.VMEM((s_rows * (NB // LANES), LANES), f32),
            pltpu.VMEM((s_rows * (NB // LANES), LANES), f32),
            pltpu.VMEM((r_rows, 2 * NB), jnp.bfloat16),
            pltpu.VMEM((COLS * SEGS, NB), f32),
            pltpu.VMEM((COLS * SEGS, NB), f32),
            pltpu.VMEM((COLS * SEGS, NB), f32),
            pltpu.VMEM((n_out * COLS, 2 * NB), jnp.bfloat16),
            pltpu.VMEM((2 * NB, LAGS), jnp.bfloat16),
            pltpu.SemaphoreType.DMA,
        ],
        name="correlate",
    )(positions, jnp.asarray(lag_table()), *sources, *receivers)


def gather(x, axis, n):
    if n > 4 or n & (n - 1):
        return [lax.all_gather(x, axis, axis=0, tiled=True)], None
    me = lax.axis_index(axis)
    blocks = [x] + [lax.ppermute(x, axis, [(i, i ^ m) for i in range(n)]) for m in range(1, n)]
    return blocks, me


def on_device(mesh_shape, traces, offsets, receiver_slots):
    chans = traces.shape[0]
    white = spectra(traces, offsets)
    sources, me_r = gather(white, "rcv", mesh_shape["rcv"])
    receivers, me_s = gather(white, "src", mesh_shape["src"])
    slots = receiver_slots[0]
    if me_s is not None:
        slots = ((slots // chans) ^ me_s) * chans + slots % chans
    order = jnp.arange(len(sources), dtype=jnp.int32)
    if me_r is not None:
        order = order ^ me_r
    positions = jnp.concatenate([order, slots])
    return correlate(sources, receivers, positions, receiver_slots.shape[1])


def solution(mesh):
    in_specs = (P(("group", "src", "rcv"), None), P("group"), P(("group", "rcv"), None))
    out_specs = P(("group", "src"), "rcv", None)
    return jax.shard_map(
        functools.partial(on_device, dict(mesh.shape)),
        mesh=mesh,
        in_specs=in_specs,
        out_specs=out_specs,
        check_vma=False,
    )
```
